256 devices in a mesh: row: 16 (over z_hi, y, core), col: 16 (over x, z_lo).
Axes of the slice: x: 4, y: 4, z: 8 (z_hi: 2, z_lo: 4; z = z_hi * 4 + z_lo), core: 2. Of those that a mesh axis runs over, the one named last changes fastest.
Arguments:
- act_sketch: bfloat16 [2, 8192, 256], P(None, 'row'), may hold values from -6 to 6
- grad_sketch: bfloat16 [2, 8192, 256], P(None, 'row'), may hold values from -6 to 6
- targets: float32 [8192, 256], P('row'), may hold values from -6 to 6
Outputs:
- residual: float32 [8192, 256], P(('row', 'col'))
The draws below stay inside these ranges and needn't reach their ends.
All inputs are finite; a program needn't handle non-finite values.
Results may differ from the reference program's by a relative error of at most 0.014.
The reference program's roundings to bfloat16 on the way (of `kernel`) count: a program that leaves them out, or rounds other values in their place, can miss the bound.
Values may be sent and summed in bfloat16 or wider, within the bound.
A program may use at most 64 MiB of HBM per device.

```python
import math
import jax
import jax.numpy as jnp
from jax import lax

W = 256
OUT = 256
LAYERS = 2
ITERS = 8
N = 8192
CB = 512


def block_levels(stream_key, extent, shards, smallest, largest):
    loudness = 1.0
    for axis_at, shards_of in shards:
        heights = jax.random.uniform(jax.random.fold_in(jax.random.fold_in(stream_key, 6), axis_at), (shards_of,), jnp.float32, smallest / len(shards), largest / len(shards))
        loudness = loudness * jnp.repeat(jnp.exp(heights), extent[axis_at] // shards_of).reshape((-1,) + (1,) * (len(extent) - 1 - axis_at))
    return loudness


def scatter_about(stream_key, shape, deviation, bound, shards=(), kind=jnp.bfloat16):
    gain = block_levels(stream_key, shape, shards, -0.22, 0.18) if shards else 1.0
    values = jax.random.normal(stream_key, shape, jnp.float32) * deviation * gain
    return jnp.minimum(jnp.maximum(values, -bound), bound).astype(kind)


def setup_inputs(seed: int = 0) -> dict:
    arg_keys = jax.random.split(jax.random.key(seed), 4)
    act_sketch = scatter_about(arg_keys[0], (LAYERS, N, W), 1.0, 6.0, ((1, 16),))
    grad_sketch = scatter_about(arg_keys[1], (LAYERS, N, W), 1.0, 6.0, ((1, 16),))
    targets = scatter_about(arg_keys[2], (N, OUT), 1.0, 6.0, ((0, 16),), jnp.float32)
    return {"act_sketch": act_sketch, "grad_sketch": grad_sketch, "targets": targets}


def reference(act_sketch, grad_sketch, targets):
    scale = W * math.sqrt(N) / 4.0
    blocks = N // CB
    act_all = act_sketch.astype(jnp.float32)
    grad_all = grad_sketch.astype(jnp.float32)

    def kernel_block(index):
        start = (index * CB).astype(jnp.int32)
        total = jnp.zeros((CB, N), jnp.float32)
        for layer in range(LAYERS):
            act_rows = lax.dynamic_slice_in_dim(act_all[layer], start, CB, 0)
            grad_rows = lax.dynamic_slice_in_dim(grad_all[layer], start, CB, 0)
            act_gram = jnp.dot(act_rows, act_all[layer].T)
            grad_gram = jnp.dot(grad_rows, grad_all[layer].T)
            total = total + act_gram * grad_gram
        return (total / scale).astype(jnp.bfloat16)
    kernel = lax.map(kernel_block, jnp.arange(blocks, dtype=jnp.int32))
    residual = targets
    for step in range(ITERS):
        squashed = jnp.tanh(residual).astype(jnp.bfloat16).astype(jnp.float32)

        def apply_block(kblock):
            return jnp.dot(kblock.astype(jnp.float32), squashed)
        update = lax.map(apply_block, kernel).reshape(N, OUT)
        residual = residual - 0.05 * update
    return residual
```

```python
import functools
import math

import jax
import jax.numpy as jnp
from jax import lax
from jax.experimental import pallas as pl
from jax.experimental.pallas import tpu as pltpu
from jax.sharding import PartitionSpec as P

ITERS = 8
CHUNKS = 4
RATE = 0.05
MESH = pl.DeviceIdType.MESH


def place(x, y, z, k):
    return ((z // 4) * 8 + y * 2 + k, x * 4 + z % 4)


def kernel(inv_scale, act, grad, tgt, out, ra, rg, ca, cg, kt, xbuf, rsend, rrecv, acc, yloc, res, tbuf, sq, osend, orecv,
           lsem, zs, zr, ts, tr, xs, xr, ys, yr, fs, fr, rss, rsr, ags, agr, oss, osr):
    row, col = lax.axis_index("row"), lax.axis_index("col")
    x, zlo = col // 4, col % 4
    hi, y, k = row // 8, (row // 2) % 4, row % 2
    z = hi * 4 + zlo
    zb = z % 2
    q = z // 2
    lo = 1 - hi
    s_me = 2 * x + zb
    j_me = 2 * y + k
    sketches = ((act, ra, ca), (grad, rg, cg))

    def at(dx=0, dy=0, dzb=0, dk=0):
        return place((x + dx) % 4, (y + dy) % 4, z + dzb * (1 - 2 * zb), k + dk * (1 - 2 * k))

    def remote(src, dst, ssem, rsem, device):
        return pltpu.make_async_remote_copy(
            src_ref=src, dst_ref=dst, send_sem=ssem, recv_sem=rsem, device_id=device, device_id_type=MESH)

    local = []
    for n, (src, r, c) in enumerate(sketches):
        local.append(pltpu.make_async_copy(src, r.at[:, :, hi], lsem.at[0, n]))
        local.append(pltpu.make_async_copy(src.at[:, s_me], c.at[:, j_me, hi], lsem.at[1, n]))
    tcols = pl.ds(pl.multiple_of((q // 2) * 128, 128), 128)
    tlocal = pltpu.make_async_copy(tgt.at[s_me, :, tcols], tbuf.at[hi], lsem.at[2, 0])
    for c in local:
        c.start()
    tlocal.start()

    sums = [(dx, dz) for dx in (2, 1, 3, 0) for dz in (1, 0) if (dx, dz) != (0, 0)]
    gathers = [(dy, dk) for dy in (2, 1, 3, 0) for dk in (1, 0) if (dy, dk) != (0, 0)]
    barrier = pltpu.get_barrier_semaphore()

    def greet(device):
        pl.semaphore_signal(barrier, inc=1, device_id=device, device_id_type=MESH)

    for dx, dz in sums:
        greet(at(dx=dx, dzb=dz))
    for dy, dk in gathers:
        greet(at(dy=dy, dk=dk))
    for n in range(1, 4):
        for b in range(2):
            greet(place(x, y, 2 * ((q + n) % 4) + b, k))
    pl.semaphore_wait(barrier, len(sums) + len(gathers) + 6)

    mirror = place(x, y, 7 - z, k)
    s_mirror = 2 * x + 1 - zb
    mcols = pl.ds(pl.multiple_of(((3 - q) // 2) * 128, 128), 128)
    tcopy = remote(tgt.at[s_mirror, :, mcols], tbuf.at[hi], ts, tr, mirror)
    tcopy.start()
    zc = []
    mine = pl.ds(2 * x, 2)
    rows_of = [pl.ds(c * (64 // CHUNKS), 64 // CHUNKS) for c in range(CHUNKS)]
    for chunk, i in enumerate(rows_of):
        zc.append([remote(src.at[:, mine, i], r.at[:, mine, hi, i], zs.at[chunk, n], zr.at[chunk, n], mirror)
                   for n, (src, r, c) in enumerate(sketches)])
    for c in zc[0]:
        c.start()
    yc, fc, xc = {}, {}, {}
    everything = pl.ds(0, 64)

    def forward(dy, part, half, i=everything):
        j = 2 * ((y - dy) % 4) + k
        fc[dy, part] = []
        for n, (src, r, c) in enumerate(sketches):
            if dy == 0:
                source = src.at[:, s_me, i] if part == 0 else r.at[:, s_me, lo, i]
            else:
                source = c.at[:, j, half, i]
            fc[dy, part].append(remote(source, c.at[:, j, half, i], fs.at[dy, part, n], fr.at[dy, part, n], at(dk=1)))
        for c in fc[dy, part]:
            c.start()

    def columns(part, half, i=everything):
        for dy in (2, 1, 3):
            yc[dy, part] = []
            for n, (src, r, c) in enumerate(sketches):
                source = src.at[:, s_me, i] if part == 0 else r.at[:, s_me, lo, i]
                yc[dy, part].append(remote(
                    source, c.at[:, j_me, half, i], ys.at[dy - 1, part, n], yr.at[dy - 1, part, n], at(dy=dy)))
            for c in yc[dy, part]:
                c.start()

    def rows(dx, chunk):
        i = rows_of[chunk]
        xc[dx, chunk] = [remote(r.at[:, mine, lo, i], r.at[:, mine, lo, i], xs.at[dx - 1, chunk, n], xr.at[dx - 1, chunk, n],
                                at(dx=dx)) for n, (src, r, c) in enumerate(sketches)]
        for c in xc[dx, chunk]:
            c.start()

    columns(0, hi)
    for chunk in zc[1:]:
        for c in chunk:
            c.start()
    forward(0, 0, hi)

    tlocal.wait()
    tcopy.wait_recv()
    sq[...] = tbuf[...].reshape(128, 128).T
    half_at = pl.multiple_of((q % 2) * 64, 64)
    res[...] = sq[pl.ds(half_at, 64), :]
    jcols = pl.ds(pl.multiple_of(j_me * 128, 128), 128)

    def gather(p):
        xbuf[p, :, jcols] = jnp.tanh(res[...]).astype(jnp.bfloat16)
        copies = [remote(xbuf.at[p, :, jcols], xbuf.at[p, :, jcols], ags.at[p, n], agr.at[p, n], at(dy=dy, dk=dk))
                  for n, (dy, dk) in enumerate(gathers)]
        for c in copies:
            c.start()
        return copies

    first = gather(0)

    for chunk, i in enumerate(rows_of):
        for c in zc[chunk]:
            c.wait_recv()
        columns(1 + chunk, lo, i)
        rows(1, chunk)
        rows(3, chunk)
        if chunk:
            rows(2, chunk - 1)
        forward(0, 1 + chunk, lo, i)
        if chunk == 1:
            for dy in (1, 3, 2):
                for c in yc[dy, 0]:
                    c.wait_recv()
                forward(dy, 0, hi)
    rows(2, CHUNKS - 1)
    for n, (src, r, c) in enumerate(sketches):
        own = pltpu.make_async_copy(r.at[:, s_me, lo], c.at[:, j_me, lo], lsem.at[3, n])
        own.start()
        local.append(own)
    for chunk, i in enumerate(rows_of):
        for dy in (1, 3, 2):
            for c in yc[dy, 1 + chunk]:
                c.wait_recv()
            forward(dy, 1 + chunk, lo, i)
    for c in local:
        c.wait()
    for group in fc.values():
        for c in group:
            c.wait_recv()

    for dx in (0, 1, 3, 2):
        if dx:
            for chunk in range(CHUNKS):
                for c in xc[dx, chunk]:
                    c.wait_recv()
        quarter = (x - dx) % 4
        lanes = pl.ds(pl.multiple_of(quarter * 256, 256), 256)

        def block(m, _):
            total = jnp.zeros((256, 256), jnp.float32)
            for layer in range(2):
                grams = []
                for src, r, c in sketches:
                    left = c[layer, pl.ds(2 * m, 2)].reshape(256, 256)
                    right = r[layer, pl.ds(2 * quarter, 2)].reshape(256, 256)
                    grams.append(lax.dot_general(left, right, (((1,), (1,)), ((), ())), preferred_element_type=jnp.float32))
                total = total + grams[0] * grams[1]
            kt[pl.ds(pl.multiple_of(m * 256, 256), 256), lanes] = (total * inv_scale).astype(jnp.bfloat16)
            return 0

        lax.fori_loop(0, 4, block, 0, unroll=True)

    tcopy.wait_send()
    for group in (*zc, *yc.values(), *fc.values(), *xc.values()):
        for c in group:
            c.wait_send()

    def step(p, last=False):
        gathered = [remote(xbuf.at[p, :, jcols], xbuf.at[p, :, jcols], ags.at[p, n], agr.at[p, n], at(dy=dy, dk=dk))
                    for n, (dy, dk) in enumerate(gathers)]
        arrived = {d: c for d, c in zip(gathers, gathered)}

        def pair_of(dy):
            return pl.ds(pl.multiple_of(((y - dy) % 4) * 256, 256), 256)

        for dy in (0, 1, 3):
            for dk in (0, 1):
                if (dy, dk) != (0, 0):
                    arrived[dy, dk].wait_recv()
            term = jnp.dot(xbuf[p, :, pair_of(dy)], kt[pair_of(dy), :], preferred_element_type=jnp.float32)
            acc[...] = term if dy == 0 else acc[...] + term
        for dk in (0, 1):
            arrived[2, dk].wait_recv()
        last_pair = xbuf[p, :, pair_of(2)]
        copies = {}
        for dx in (2, 1, 3, 0):
            lanes = pl.ds(pl.multiple_of(((x + dx) % 4) * 256, 256), 256)
            part = acc[:, lanes] + jnp.dot(last_pair, kt[pair_of(2), lanes], preferred_element_type=jnp.float32)
            for b in range(2):
                rsend[p, dx, b] = part[:, b * 128:(b + 1) * 128].astype(jnp.bfloat16)
            if dx == 0:
                yloc[...] = part
            for n, (ddx, dz) in enumerate(sums):
                if ddx == dx:
                    copies[n] = remote(rsend.at[p, dx, zb + dz * (1 - 2 * zb)], rrecv.at[p, n], rss.at[p, n], rsr.at[p, n],
                                       at(dx=dx, dzb=dz))
                    copies[n].start()
        for c in gathered:
            c.wait_send()
        total = yloc[:, pl.ds(pl.multiple_of(zb * 128, 128), 128)]
        for n in reversed(range(7)):
            copies[n].wait_recv()
            total = total + rrecv[p, n].astype(jnp.float32)
        res[...] = res[...] - RATE * total
        if not last:
            gather(1 - p)
        for c in copies.values():
            c.wait_send()

    def pair(_, carry):
        step(0)
        step(1)
        return carry

    lax.fori_loop(0, ITERS // 2 - 1, pair, 0)
    step(0)
    step(1, last=True)

    sq[...] = jnp.zeros_like(sq)
    sq[pl.ds(half_at, 64), :] = res[...]
    osend[...] = sq[...].T
    for h in range(2):
        for e in range(2):
            n = 2 * h + e
            z_to = 4 * h + 2 * zb + e
            piece = osend.at[pl.ds(h * 64 + e * 32, 32)]

            @pl.when(z_to != z)
            def _():
                remote(piece, orecv.at[q], oss.at[n], osr.at[q], place(x, y, z_to, k)).start()

            @pl.when(z_to == z)
            def _():
                pltpu.make_async_copy(piece, orecv.at[q], osr.at[q]).start()
    for n in range(4):
        pltpu.make_async_copy(osend.at[pl.ds(0, 32)], orecv.at[n], osr.at[n]).wait()
    out[:, 0:128] = orecv[0] + orecv[1]
    out[:, 128:256] = orecv[2] + orecv[3]
    for h in range(2):
        for e in range(2):
            n = 2 * h + e
            z_to = 4 * h + 2 * zb + e
            piece = osend.at[pl.ds(h * 64 + e * 32, 32)]

            @pl.when(z_to != z)
            def _():
                remote(piece, orecv.at[q], oss.at[n], osr.at[q], place(x, y, z_to, k)).wait_send()


def body(act_sketch, grad_sketch, targets):
    layers, examples, width = act_sketch.shape
    inv_scale = 4.0 / (width * math.sqrt(examples * lax.axis_size("row")))
    bf16, f32 = jnp.bfloat16, jnp.float32
    dma = pltpu.SemaphoreType.DMA
    hbm = pl.BlockSpec(memory_space=pltpu.HBM)
    return pl.pallas_call(
        functools.partial(kernel, inv_scale),
        name="descent",
        out_shape=jax.ShapeDtypeStruct((32, 256), f32),
        in_specs=[hbm, hbm, hbm],
        out_specs=pl.BlockSpec(memory_space=pltpu.VMEM),
        scratch_shapes=[
            *[pltpu.VMEM((2, 8, 2, 64, 256), bf16)] * 4,
            pltpu.VMEM((1024, 1024), bf16),
            pltpu.VMEM((2, 64, 1024), bf16),
            pltpu.VMEM((2, 4, 2, 64, 128), bf16),
            pltpu.VMEM((2, 7, 64, 128), bf16),
            pltpu.VMEM((64, 1024), f32),
            pltpu.VMEM((64, 256), f32),
            pltpu.VMEM((64, 128), f32),
            pltpu.VMEM((2, 64, 128), f32),
            pltpu.VMEM((128, 128), f32),
            pltpu.VMEM((128, 128), f32),
            pltpu.VMEM((4, 32, 128), f32),
            dma((4, 2)),
            dma((CHUNKS, 2)), dma((CHUNKS, 2)),
            dma(()), dma(()),
            dma((3, CHUNKS, 2)), dma((3, CHUNKS, 2)),
            dma((3, 1 + CHUNKS, 2)), dma((3, 1 + CHUNKS, 2)),
            dma((4, 1 + CHUNKS, 2)), dma((4, 1 + CHUNKS, 2)),
            dma((2, 7)), dma((2, 7)),
            dma((2, 7)), dma((2, 7)),
            dma((4,)), dma((4,)),
        ],
        compiler_params=pltpu.CompilerParams(collective_id=0, has_side_effects=True, vmem_limit_bytes=40 * 2**20),
    )(*[pltpu.with_memory_space_constraint(v, pltpu.HBM) for v in (act_sketch.reshape(layers, 8, 64, width), grad_sketch.reshape(layers, 8, 64, width),
      targets.reshape(8, 64, targets.shape[1]))])


def solution(mesh):
    return jax.shard_map(
        body,
        mesh=mesh,
        in_specs=(P(None, "row", None), P(None, "row", None), P("row", None)),
        out_specs=P(("row", "col"), None),
        check_vma=False,
    )
```

```python
import functools
import math

import jax
import jax.numpy as jnp
from jax import lax
from jax.experimental import pallas as pl
from jax.experimental.pallas import tpu as pltpu
from jax.sharding import PartitionSpec as P

ITERS = 8
CHUNKS = 4
ORDER = ((2,), (3,), (0, 1))
RATE = 0.05
MESH = pl.DeviceIdType.MESH


def place(x, y, z, k):
    return ((z // 4) * 8 + y * 2 + k, x * 4 + z % 4)


def kernel(inv_scale, act, grad, tgt, out, ra, rg, ca, cg, kt, xbuf, rsend, rrecv, acc, yloc, res, tbuf, sq, osend, orecv,
           lsem, zs, zfs, zr, ts, tr, xs, xr, ys, yr, fs, fr, rss, rsr, ags, agr, oss, osr):
    row, col = lax.axis_index("row"), lax.axis_index("col")
    x, zlo = col // 4, col % 4
    hi, y, k = row // 8, (row // 2) % 4, row % 2
    z = hi * 4 + zlo
    zb = z % 2
    q = z // 2
    lo = 1 - hi
    s_me = 2 * x + zb
    j_me = 2 * y + k
    sketches = ((act, ra, ca), (grad, rg, cg))

    def at(dx=0, dy=0, dzb=0, dk=0):
        return place((x + dx) % 4, (y + dy) % 4, z + dzb * (1 - 2 * zb), k + dk * (1 - 2 * k))

    def remote(src, dst, ssem, rsem, device):
        return pltpu.make_async_remote_copy(
            src_ref=src, dst_ref=dst, send_sem=ssem, recv_sem=rsem, device_id=device, device_id_type=MESH)

    local = []
    for n, (src, r, c) in enumerate(sketches):
        local.append(pltpu.make_async_copy(src, r.at[:, :, hi], lsem.at[0, n]))
        local.append(pltpu.make_async_copy(src.at[:, s_me], c.at[:, j_me, hi], lsem.at[1, n]))
    tcols = pl.ds(pl.multiple_of((q // 2) * 128, 128), 128)
    tlocal = pltpu.make_async_copy(tgt.at[s_me, :, tcols], tbuf.at[hi], lsem.at[2, 0])
    for c in local:
        c.start()
    tlocal.start()

    sums = [(dx, dz) for dx in (2, 1, 3, 0) for dz in (1, 0) if (dx, dz) != (0, 0)]
    gathers = [(dy, dk) for dy in (2, 1, 3, 0) for dk in (1, 0) if (dy, dk) != (0, 0)]
    barrier = pltpu.get_barrier_semaphore()

    def greet(device):
        pl.semaphore_signal(barrier, inc=1, device_id=device, device_id_type=MESH)

    for n in range(1, 4):
        for b in range(2):
            greet(place(x, y, 2 * ((q + n) % 4) + b, k))
    for dx, dz in sums:
        greet(at(dx=dx, dzb=dz))
    for dy, dk in gathers:
        greet(at(dy=dy, dk=dk))
    pl.semaphore_wait(barrier, len(sums) + len(gathers) + 6)

    mirror = place(x, y, 7 - z, k)
    s_mirror = 2 * x + 1 - zb
    mcols = pl.ds(pl.multiple_of(((3 - q) // 2) * 128, 128), 128)
    tcopy = remote(tgt.at[s_mirror, :, mcols], tbuf.at[hi], ts, tr, mirror)
    tcopy.start()
    outer = zlo % 3 == 0
    mine = pl.ds(2 * x, 2)
    rows_of = [pl.ds(c * (64 // CHUNKS), 64 // CHUNKS) for c in range(CHUNKS)]
    zc, zf = [], []
    for chunk, i in enumerate(rows_of):
        zc.append([remote(src.at[:, mine, i], r.at[:, mine, hi, i], zs.at[chunk, n], zr.at[chunk, n], mirror)
                   for n, (src, r, c) in enumerate(sketches)])
        zf.append([remote(r.at[:, mine, lo, i], r.at[:, mine, lo, i], zfs.at[chunk, n], zr.at[chunk, n], at(dzb=1))
                   for n, (src, r, c) in enumerate(sketches)])

    @pl.when(outer)
    def _():
        for c in (c for group in zc for c in group):
            c.start()

    yc, fc, xc = {}, {}, {}
    everything = pl.ds(0, 64)

    def forward(dy, part, half, i=everything):
        j = 2 * ((y - dy) % 4) + k
        fc[dy, part] = []
        for n, (src, r, c) in enumerate(sketches):
            if dy == 0:
                source = src.at[:, s_me, i] if part == 0 else r.at[:, s_me, lo, i]
            else:
                source = c.at[:, j, half, i]
            fc[dy, part].append(remote(source, c.at[:, j, half, i], fs.at[dy, part, n], fr.at[dy, part, n], at(dk=1)))
        for c in fc[dy, part]:
            c.start()

    def columns(part, half, i=everything):
        for dy in (2, 1, 3):
            yc[dy, part] = []
            for n, (src, r, c) in enumerate(sketches):
                source = src.at[:, s_me, i] if part == 0 else r.at[:, s_me, lo, i]
                yc[dy, part].append(remote(
                    source, c.at[:, j_me, half, i], ys.at[dy - 1, part, n], yr.at[dy - 1, part, n], at(dy=dy)))
            for c in yc[dy, part]:
                c.start()

    def rows(dx, chunk):
        i = rows_of[chunk]
        xc[dx, chunk] = [remote(r.at[:, mine, lo, i], r.at[:, mine, lo, i], xs.at[dx - 1, chunk, n], xr.at[dx - 1, chunk, n],
                                at(dx=dx)) for n, (src, r, c) in enumerate(sketches)]
        for c in xc[dx, chunk]:
            c.start()

    columns(0, hi)
    forward(0, 0, hi)

    tlocal.wait()
    tcopy.wait_recv()
    sq[...] = tbuf[...].reshape(128, 128).T
    half_at = pl.multiple_of((q % 2) * 64, 64)
    res[...] = sq[pl.ds(half_at, 64), :]
    def slot(d):
        return pl.ds((2 * d[0] + d[1]) * 128, 128)

    def gather_copies(p):
        return [remote(xbuf.at[p, :, slot((0, 0))], xbuf.at[p, :, slot(d)], ags.at[p, n], agr.at[p, n], at(dy=d[0], dk=d[1]))
                for n, d in enumerate(gathers)]

    def gather(p):
        xbuf[p, :, slot((0, 0))] = jnp.tanh(res[...]).astype(jnp.bfloat16)
        for c in gather_copies(p):
            c.start()

    gather(0)

    for chunk, i in enumerate(rows_of):
        for c in zc[chunk]:
            c.wait_recv()

        @pl.when(outer)
        def _():
            for passed in zf[chunk]:
                passed.start()

        for dx in (2, 1, 3):
            rows(dx, chunk)
        columns(1 + chunk, lo, i)
        forward(0, 1 + chunk, lo, i)
        if chunk == 1:
            for dy in (1, 3, 2):
                for c in yc[dy, 0]:
                    c.wait_recv()
                forward(dy, 0, hi)
    for n, (src, r, c) in enumerate(sketches):
        own = pltpu.make_async_copy(r.at[:, s_me, lo], c.at[:, j_me, lo], lsem.at[3, n])
        own.start()
        local.append(own)
    for chunk, i in enumerate(rows_of):
        for dy in (1, 3, 2):
            for c in yc[dy, 1 + chunk]:
                c.wait_recv()
            forward(dy, 1 + chunk, lo, i)
    for c in local:
        c.wait()
    for group in fc.values():
        for c in group:
            c.wait_recv()

    for dx in (0, 1, 3, 2):
        if dx:
            for chunk in range(CHUNKS):
                for c in xc[dx, chunk]:
                    c.wait_recv()
        to = (4 - dx) % 4
        lanes = pl.ds(to * 256, 256)
        right_at = [2 * ((x - dx) % 4) + zb, 2 * ((x - dx) % 4) + 1 - zb]
        for dy in range(4):
            left_at = [2 * ((y - dy) % 4) + k, 2 * ((y - dy) % 4) + 1 - k]
            total = jnp.zeros((256, 256), jnp.float32)
            for layer in range(2):
                grams = []
                for src, r, c in sketches:
                    left = jnp.concatenate([c[layer, j].reshape(128, 256) for j in left_at], axis=0)
                    right = jnp.concatenate([r[layer, j].reshape(128, 256) for j in right_at], axis=0)
                    grams.append(lax.dot_general(left, right, (((1,), (1,)), ((), ())), preferred_element_type=jnp.float32))
                total = total + grams[0] * grams[1]
            kt[pl.ds(dy * 256, 256), lanes] = (total * inv_scale).astype(jnp.bfloat16)

    tcopy.wait_send()

    @pl.when(outer)
    def _():
        for c in (c for group in (*zc, *zf) for c in group):
            c.wait_send()

    for group in (*yc.values(), *fc.values(), *xc.values()):
        for c in group:
            c.wait_send()

    def step(p, last=False):
        gathered = gather_copies(p)
        arrived = dict(zip(gathers, gathered))
        for d in ((0, 1), (1, 0), (1, 1), (3, 0), (3, 1)):
            arrived[d].wait_recv()
        term = jnp.dot(xbuf[p, :, 0:512], kt[0:512, :], preferred_element_type=jnp.float32)
        acc[...] = term + jnp.dot(xbuf[p, :, 768:1024], kt[768:1024, :], preferred_element_type=jnp.float32)
        for d in ((2, 0), (2, 1)):
            arrived[d].wait_recv()
        last_pair = xbuf[p, :, 512:768]
        copies = {}
        for group in ORDER:
            first, count = group[0] * 256, len(group) * 256
            part = acc[:, first:first + count] + jnp.dot(
                last_pair, kt[512:768, first:first + count], preferred_element_type=jnp.float32)
            if 0 in group:
                yloc[...] = part[:, 0:128]
            for at_n, (dx, dz) in enumerate((dx, dz) for dx in group for dz in range(2)):
                if (dx, dz) != (0, 0):
                    n = sums.index((dx, dz))
                    rsend[p, n] = part[:, at_n * 128:(at_n + 1) * 128].astype(jnp.bfloat16)
                    copies[n] = remote(rsend.at[p, n], rrecv.at[p, n], rss.at[p, n], rsr.at[p, n], at(dx=dx, dzb=dz))
            for n in sorted(copies):
                if sums[n][0] in group:
                    copies[n].start()
        for c in gathered:
            c.wait_send()
        total = yloc[...]
        for n in reversed(range(7)):
            copies[n].wait_recv()
            total = total + rrecv[p, n].astype(jnp.float32)
        res[...] = res[...] - RATE * total
        if not last:
            gather(1 - p)
        for c in copies.values():
            c.wait_send()

    def pair(_, carry):
        step(0)
        step(1)
        return carry

    lax.fori_loop(0, ITERS // 2 - 1, pair, 0)
    step(0)
    step(1, last=True)

    sq[...] = jnp.zeros_like(sq)
    sq[pl.ds(half_at, 64), :] = res[...]
    osend[...] = sq[...].T
    for h in range(2):
        for e in range(2):
            n = 2 * h + e
            z_to = 4 * h + 2 * zb + e
            piece = osend.at[pl.ds(h * 64 + e * 32, 32)]

            @pl.when(z_to != z)
            def _():
                remote(piece, orecv.at[q], oss.at[n], osr.at[q], place(x, y, z_to, k)).start()

            @pl.when(z_to == z)
            def _():
                pltpu.make_async_copy(piece, orecv.at[q], osr.at[q]).start()
    for n in range(4):
        pltpu.make_async_copy(osend.at[pl.ds(0, 32)], orecv.at[n], osr.at[n]).wait()
    out[:, 0:128] = orecv[0] + orecv[1]
    out[:, 128:256] = orecv[2] + orecv[3]
    for h in range(2):
        for e in range(2):
            n = 2 * h + e
            z_to = 4 * h + 2 * zb + e
            piece = osend.at[pl.ds(h * 64 + e * 32, 32)]

            @pl.when(z_to != z)
            def _():
                remote(piece, orecv.at[q], oss.at[n], osr.at[q], place(x, y, z_to, k)).wait_send()


def body(act_sketch, grad_sketch, targets):
    layers, examples, width = act_sketch.shape
    inv_scale = 4.0 / (width * math.sqrt(examples * lax.axis_size("row")))
    bf16, f32 = jnp.bfloat16, jnp.float32
    dma = pltpu.SemaphoreType.DMA
    hbm = pl.BlockSpec(memory_space=pltpu.HBM)
    return pl.pallas_call(
        functools.partial(kernel, inv_scale),
        name="descent",
        out_shape=jax.ShapeDtypeStruct((32, 256), f32),
        in_specs=[hbm, hbm, hbm],
        out_specs=pl.BlockSpec(memory_space=pltpu.VMEM),
        scratch_shapes=[
            *[pltpu.VMEM((2, 8, 2, 64, 256), bf16)] * 4,
            pltpu.VMEM((1024, 1024), bf16),
            pltpu.VMEM((2, 64, 1024), bf16),
            pltpu.VMEM((2, 7, 64, 128), bf16),
            pltpu.VMEM((2, 7, 64, 128), bf16),
            pltpu.VMEM((64, 1024), f32),
            pltpu.VMEM((64, 128), f32),
            pltpu.VMEM((64, 128), f32),
            pltpu.VMEM((2, 64, 128), f32),
            pltpu.VMEM((128, 128), f32),
            pltpu.VMEM((128, 128), f32),
            pltpu.VMEM((4, 32, 128), f32),
            dma((4, 2)),
            dma((CHUNKS, 2)), dma((CHUNKS, 2)), dma((CHUNKS, 2)),
            dma(()), dma(()),
            dma((3, CHUNKS, 2)), dma((3, CHUNKS, 2)),
            dma((3, 1 + CHUNKS, 2)), dma((3, 1 + CHUNKS, 2)),
            dma((4, 1 + CHUNKS, 2)), dma((4, 1 + CHUNKS, 2)),
            dma((2, 7)), dma((2, 7)),
            dma((2, 7)), dma((2, 7)),
            dma((4,)), dma((4,)),
        ],
        compiler_params=pltpu.CompilerParams(collective_id=0, has_side_effects=True, vmem_limit_bytes=40 * 2**20),
    )(*[pltpu.with_memory_space_constraint(v, pltpu.HBM) for v in (act_sketch.reshape(layers, 8, 64, width), grad_sketch.reshape(layers, 8, 64, width),
      targets.reshape(8, 64, targets.shape[1]))])


def solution(mesh):
    return jax.shard_map(
        body,
        mesh=mesh,
        in_specs=(P(None, "row", None), P(None, "row", None), P("row", None)),
        out_specs=P(("row", "col"), None),
        check_vma=False,
    )
```

```python
import functools
import math

import jax
import jax.numpy as jnp
from jax import lax
from jax.experimental import pallas as pl
from jax.experimental.pallas import tpu as pltpu
from jax.sharding import PartitionSpec as P

ITERS = 8
CHUNKS = 4
HALVES = 2
RATE = 0.05
MESH = pl.DeviceIdType.MESH


def place(x, y, z, k):
    return ((z // 4) * 8 + y * 2 + k, x * 4 + z % 4)


def kernel(inv_scale, act, grad, tgt, out, ra, rg, ca, cg, kt, xbuf, rsend, rrecv, yloc, res, tbuf, sq, osend, orecv,
           lsem, zs, zfs, zr, ts, tr, xs, xr, ys, yr, fs, fr, rss, rsr, ags, agr, oss, osr):
    row, col = lax.axis_index("row"), lax.axis_index("col")
    x, zlo = col // 4, col % 4
    hi, y, k = row // 8, (row // 2) % 4, row % 2
    z = hi * 4 + zlo
    zb = z % 2
    q = z // 2
    lo = 1 - hi
    s_me = 2 * x + zb
    j_me = 2 * y + k
    sketches = ((act, ra, ca), (grad, rg, cg))

    def at(dx=0, dy=0, dzb=0, dk=0):
        return place((x + dx) % 4, (y + dy) % 4, z + dzb * (1 - 2 * zb), k + dk * (1 - 2 * k))

    def remote(src, dst, ssem, rsem, device):
        return pltpu.make_async_remote_copy(
            src_ref=src, dst_ref=dst, send_sem=ssem, recv_sem=rsem, device_id=device, device_id_type=MESH)

    local = []
    for n, (src, r, c) in enumerate(sketches):
        local.append(pltpu.make_async_copy(src, r.at[:, :, hi], lsem.at[0, n]))
        local.append(pltpu.make_async_copy(src.at[:, s_me], c.at[:, j_me, hi], lsem.at[1, n]))
    tcols = pl.ds(pl.multiple_of((q // 2) * 128, 128), 128)
    tlocal = pltpu.make_async_copy(tgt.at[s_me, :, tcols], tbuf.at[hi], lsem.at[2, 0])
    for c in local:
        c.start()
    tlocal.start()

    sums = [(dx, dz) for dx in (2, 1, 3, 0) for dz in (1, 0) if (dx, dz) != (0, 0)]
    gathers = [(dy, dk) for dy in (2, 1, 3, 0) for dk in (1, 0) if (dy, dk) != (0, 0)]
    barrier = pltpu.get_barrier_semaphore()

    def greet(device):
        pl.semaphore_signal(barrier, inc=1, device_id=device, device_id_type=MESH)

    for n in range(1, 4):
        for b in range(2):
            greet(place(x, y, 2 * ((q + n) % 4) + b, k))
    for dx, dz in sums:
        greet(at(dx=dx, dzb=dz))
    for dy, dk in gathers:
        greet(at(dy=dy, dk=dk))
    pl.semaphore_wait(barrier, len(sums) + len(gathers) + 6)

    mirror = place(x, y, 7 - z, k)
    s_mirror = 2 * x + 1 - zb
    mcols = pl.ds(pl.multiple_of(((3 - q) // 2) * 128, 128), 128)
    tcopy = remote(tgt.at[s_mirror, :, mcols], tbuf.at[hi], ts, tr, mirror)
    tcopy.start()
    outer = zlo % 3 == 0
    mine = pl.ds(2 * x, 2)
    rows_of = [pl.ds(c * (64 // CHUNKS), 64 // CHUNKS) for c in range(CHUNKS)]
    zc, zf = [], []
    for chunk, i in enumerate(rows_of):
        zc.append([remote(src.at[:, mine, i], r.at[:, mine, hi, i], zs.at[chunk, n], zr.at[chunk, n], mirror)
                   for n, (src, r, c) in enumerate(sketches)])
        zf.append([remote(r.at[:, mine, lo, i], r.at[:, mine, lo, i], zfs.at[chunk, n], zr.at[chunk, n], at(dzb=1))
                   for n, (src, r, c) in enumerate(sketches)])

    @pl.when(outer)
    def _():
        for c in (c for group in zc for c in group):
            c.start()

    yc, fc, xc = {}, {}, {}
    everything = pl.ds(0, 64)

    def forward(dy, part, half, i=everything):
        j = 2 * ((y - dy) % 4) + k
        fc[dy, part] = []
        for n, (src, r, c) in enumerate(sketches):
            if dy == 0:
                source = src.at[:, s_me, i] if part == 0 else r.at[:, s_me, lo, i]
            else:
                source = c.at[:, j, half, i]
            fc[dy, part].append(remote(source, c.at[:, j, half, i], fs.at[dy, part, n], fr.at[dy, part, n], at(dk=1)))
        for c in fc[dy, part]:
            c.start()

    def columns(part, half, i=everything):
        for dy in (2, 1, 3):
            yc[dy, part] = []
            for n, (src, r, c) in enumerate(sketches):
                source = src.at[:, s_me, i] if part == 0 else r.at[:, s_me, lo, i]
                yc[dy, part].append(remote(
                    source, c.at[:, j_me, half, i], ys.at[dy - 1, part, n], yr.at[dy - 1, part, n], at(dy=dy)))
            for c in yc[dy, part]:
                c.start()

    def rows(dx, chunk):
        i = rows_of[chunk]
        xc[dx, chunk] = [remote(r.at[:, mine, lo, i], r.at[:, mine, lo, i], xs.at[dx - 1, chunk, n], xr.at[dx - 1, chunk, n],
                                at(dx=dx)) for n, (src, r, c) in enumerate(sketches)]
        for c in xc[dx, chunk]:
            c.start()

    columns(0, hi)
    forward(0, 0, hi)

    tlocal.wait()
    tcopy.wait_recv()
    sq[...] = tbuf[...].reshape(128, 128).T
    half_at = pl.multiple_of((q % 2) * 64, 64)
    res[...] = sq[pl.ds(half_at, 64), :].reshape(res.shape)
    def slot(d):
        return pl.ds((2 * d[0] + d[1]) * 128, 128)

    def gather_copies(p, h):
        return [remote(xbuf.at[p, h, :, slot((0, 0))], xbuf.at[p, h, :, slot(d)], ags.at[p, h, n], agr.at[p, h, n],
                       at(dy=d[0], dk=d[1])) for n, d in enumerate(gathers)]

    def gather(p, h):
        xbuf[p, h, :, slot((0, 0))] = jnp.tanh(res[h]).astype(jnp.bfloat16)
        for c in gather_copies(p, h):
            c.start()

    for h in range(HALVES):
        gather(0, h)

    for chunk, i in enumerate(rows_of):
        for c in zc[chunk]:
            c.wait_recv()

        @pl.when(outer)
        def _():
            for passed in zf[chunk]:
                passed.start()

        for dx in (2, 1, 3):
            rows(dx, chunk)
        columns(1 + chunk, lo, i)
        forward(0, 1 + chunk, lo, i)
        if chunk == 1:
            for dy in (1, 3, 2):
                for c in yc[dy, 0]:
                    c.wait_recv()
                forward(dy, 0, hi)
    for n, (src, r, c) in enumerate(sketches):
        own = pltpu.make_async_copy(r.at[:, s_me, lo], c.at[:, j_me, lo], lsem.at[3, n])
        own.start()
        local.append(own)
    for chunk, i in enumerate(rows_of):
        for dy in (1, 3, 2):
            for c in yc[dy, 1 + chunk]:
                c.wait_recv()
            forward(dy, 1 + chunk, lo, i)
    for c in local:
        c.wait()
    for group in fc.values():
        for c in group:
            c.wait_recv()

    for dx in (0, 1, 3, 2):
        if dx:
            for chunk in range(CHUNKS):
                for c in xc[dx, chunk]:
                    c.wait_recv()
        to = (4 - dx) % 4
        lanes = pl.ds(to * 256, 256)
        right_at = [2 * ((x - dx) % 4) + zb, 2 * ((x - dx) % 4) + 1 - zb]
        for dy in range(4):
            left_at = [2 * ((y - dy) % 4) + k, 2 * ((y - dy) % 4) + 1 - k]
            total = jnp.zeros((256, 256), jnp.float32)
            for layer in range(2):
                grams = []
                for src, r, c in sketches:
                    left = jnp.concatenate([c[layer, j].reshape(128, 256) for j in left_at], axis=0)
                    right = jnp.concatenate([r[layer, j].reshape(128, 256) for j in right_at], axis=0)
                    grams.append(lax.dot_general(left, right, (((1,), (1,)), ((), ())), preferred_element_type=jnp.float32))
                total = total + grams[0] * grams[1]
            kt[pl.ds(dy * 256, 256), lanes] = (total * inv_scale).astype(jnp.bfloat16)

    def step(p, last=False):
        gathered, copies = [], []
        for h in range(HALVES):
            gathered.append(gather_copies(p, h))
            for c in reversed(gathered[h]):
                c.wait_recv()
            part = jnp.dot(xbuf[p, h], kt[...], preferred_element_type=jnp.float32)
            yloc[h] = part[:, 0:128]
            copies.append([])
            for n, (dx, dz) in enumerate(sums):
                lane = (2 * dx + dz) * 128
                rsend[p, h, n] = part[:, lane:lane + 128].astype(jnp.bfloat16)
                copies[h].append(remote(
                    rsend.at[p, h, n], rrecv.at[p, h, n], rss.at[p, h, n], rsr.at[p, h, n], at(dx=dx, dzb=dz)))
            for c in copies[h]:
                c.start()
        for c in (c for group in gathered for c in group):
            c.wait_send()
        for h in range(HALVES):
            for c in reversed(copies[h]):
                c.wait_recv()
            total = yloc[h]
            for n in range(7):
                total = total + rrecv[p, h, n].astype(jnp.float32)
            res[h] = res[h] - RATE * total
            if not last:
                gather(1 - p, h)
        for c in (c for group in copies for c in group):
            c.wait_send()

    def pair(_, carry):
        step(0)
        step(1)
        return carry

    lax.fori_loop(0, ITERS // 2 - 1, pair, 0)
    step(0)
    step(1, last=True)

    sq[...] = jnp.zeros_like(sq)
    sq[pl.ds(half_at, 64), :] = res[...].reshape(64, 128)
    osend[...] = sq[...].T
    for h in range(2):
        for e in range(2):
            n = 2 * h + e
            z_to = 4 * h + 2 * zb + e
            piece = osend.at[pl.ds(h * 64 + e * 32, 32)]

            @pl.when(z_to != z)
            def _():
                remote(piece, orecv.at[q], oss.at[n], osr.at[q], place(x, y, z_to, k)).start()

            @pl.when(z_to == z)
            def _():
                pltpu.make_async_copy(piece, orecv.at[q], osr.at[q]).start()
    tcopy.wait_send()

    @pl.when(outer)
    def _():
        for c in (c for group in (*zc, *zf) for c in group):
            c.wait_send()

    for group in (*yc.values(), *fc.values(), *xc.values()):
        for c in group:
            c.wait_send()

    for n in range(4):
        pltpu.make_async_copy(osend.at[pl.ds(0, 32)], orecv.at[n], osr.at[n]).wait()
    out[:, 0:128] = orecv[0] + orecv[1]
    out[:, 128:256] = orecv[2] + orecv[3]
    for h in range(2):
        for e in range(2):
            n = 2 * h + e
            z_to = 4 * h + 2 * zb + e
            piece = osend.at[pl.ds(h * 64 + e * 32, 32)]

            @pl.when(z_to != z)
            def _():
                remote(piece, orecv.at[q], oss.at[n], osr.at[q], place(x, y, z_to, k)).wait_send()


def body(act_sketch, grad_sketch, targets):
    layers, examples, width = act_sketch.shape
    inv_scale = 4.0 / (width * math.sqrt(examples * lax.axis_size("row")))
    bf16, f32 = jnp.bfloat16, jnp.float32
    dma = pltpu.SemaphoreType.DMA
    hbm = pl.BlockSpec(memory_space=pltpu.HBM)
    return pl.pallas_call(
        functools.partial(kernel, inv_scale),
        name="descent",
        out_shape=jax.ShapeDtypeStruct((32, 256), f32),
        in_specs=[hbm, hbm, hbm],
        out_specs=pl.BlockSpec(memory_space=pltpu.VMEM),
        scratch_shapes=[
            *[pltpu.VMEM((2, 8, 2, 64, 256), bf16)] * 4,
            pltpu.VMEM((1024, 1024), bf16),
            pltpu.VMEM((2, HALVES, 64 // HALVES, 1024), bf16),
            pltpu.VMEM((2, HALVES, 7, 64 // HALVES, 128), bf16),
            pltpu.VMEM((2, HALVES, 7, 64 // HALVES, 128), bf16),
            pltpu.VMEM((HALVES, 64 // HALVES, 128), f32),
            pltpu.VMEM((HALVES, 64 // HALVES, 128), f32),
            pltpu.VMEM((2, 64, 128), f32),
            pltpu.VMEM((128, 128), f32),
            pltpu.VMEM((128, 128), f32),
            pltpu.VMEM((4, 32, 128), f32),
            dma((4, 2)),
            dma((CHUNKS, 2)), dma((CHUNKS, 2)), dma((CHUNKS, 2)),
            dma(()), dma(()),
            dma((3, CHUNKS, 2)), dma((3, CHUNKS, 2)),
            dma((3, 1 + CHUNKS, 2)), dma((3, 1 + CHUNKS, 2)),
            dma((4, 1 + CHUNKS, 2)), dma((4, 1 + CHUNKS, 2)),
            dma((2, HALVES, 7)), dma((2, HALVES, 7)),
            dma((2, HALVES, 7)), dma((2, HALVES, 7)),
            dma((4,)), dma((4,)),
        ],
        compiler_params=pltpu.CompilerParams(collective_id=0, has_side_effects=True, vmem_limit_bytes=40 * 2**20),
    )(*[pltpu.with_memory_space_constraint(v, pltpu.HBM) for v in (act_sketch.reshape(layers, 8, 64, width), grad_sketch.reshape(layers, 8, 64, width),
      targets.reshape(8, 64, targets.shape[1]))])


def solution(mesh):
    return jax.shard_map(
        body,
        mesh=mesh,
        in_specs=(P(None, "row", None), P(None, "row", None), P("row", None)),
        out_specs=P(("row", "col"), None),
        check_vma=False,
    )
```

```python
import functools
import math

import jax
import jax.numpy as jnp
from jax import lax
from jax.experimental import pallas as pl
from jax.experimental.pallas import tpu as pltpu
from jax.sharding import PartitionSpec as P

ITERS = 8
SIZES = (16, 16, 16, 16)
CHUNKS = len(SIZES)
PARTS = 4
RATE = 0.05
MESH = pl.DeviceIdType.MESH


def place(x, y, z, k):
    return ((z // 4) * 8 + y * 2 + k, x * 4 + z % 4)


def kernel(inv_scale, act, grad, tgt, out, ra, rg, ca, cg, kt, xbuf, rsend, rrecv, yloc, res, tbuf, sq, osend, orecv,
           lsem, zs, zfs, zr, ts, tr, xs, xr, ys, yr, fs, fr, rss, rsr, ags, agr, oss, osr):
    row, col = lax.axis_index("row"), lax.axis_index("col")
    x, zlo = col // 4, col % 4
    hi, y, k = row // 8, (row // 2) % 4, row % 2
    z = hi * 4 + zlo
    zb = z % 2
    q = z // 2
    lo = 1 - hi
    s_me = 2 * x + zb
    j_me = 2 * y + k
    sketches = ((act, ra, ca), (grad, rg, cg))

    def at(dx=0, dy=0, dzb=0, dk=0):
        return place((x + dx) % 4, (y + dy) % 4, z + dzb * (1 - 2 * zb), k + dk * (1 - 2 * k))

    def remote(src, dst, ssem, rsem, device):
        return pltpu.make_async_remote_copy(
            src_ref=src, dst_ref=dst, send_sem=ssem, recv_sem=rsem, device_id=device, device_id_type=MESH)

    local = []
    for n, (src, r, c) in enumerate(sketches):
        local.append(pltpu.make_async_copy(src, r.at[:, :, hi], lsem.at[0, n]))
        local.append(pltpu.make_async_copy(src.at[:, s_me], c.at[:, j_me, hi], lsem.at[1, n]))
    tcols = pl.ds(pl.multiple_of((q // 2) * 128, 128), 128)
    tlocal = pltpu.make_async_copy(tgt.at[s_me, :, tcols], tbuf.at[hi], lsem.at[2, 0])
    for c in local:
        c.start()
    tlocal.start()

    sums = [(dx, dz) for dx in (2, 1, 3, 0) for dz in (1, 0) if (dx, dz) != (0, 0)]
    gathers = [(dy, dk) for dy in (2, 1, 3, 0) for dk in (1, 0) if (dy, dk) != (0, 0)]
    barrier = pltpu.get_barrier_semaphore()

    def greet(device):
        pl.semaphore_signal(barrier, inc=1, device_id=device, device_id_type=MESH)

    for n in range(1, 4):
        for b in range(2):
            greet(place(x, y, 2 * ((q + n) % 4) + b, k))
    for dx, dz in sums:
        greet(at(dx=dx, dzb=dz))
    for dy, dk in gathers:
        greet(at(dy=dy, dk=dk))
    pl.semaphore_wait(barrier, len(sums) + len(gathers) + 6)

    mirror = place(x, y, 7 - z, k)
    s_mirror = 2 * x + 1 - zb
    mcols = pl.ds(pl.multiple_of(((3 - q) // 2) * 128, 128), 128)
    tcopy = remote(tgt.at[s_mirror, :, mcols], tbuf.at[hi], ts, tr, mirror)
    tcopy.start()
    outer = zlo % 3 == 0
    mine = pl.ds(2 * x, 2)
    rows_of = [pl.ds(sum(SIZES[:c]), SIZES[c]) for c in range(CHUNKS)]
    zc, zf = [], []
    for chunk, i in enumerate(rows_of):
        zc.append([remote(src.at[:, mine, i], r.at[:, mine, hi, i], zs.at[chunk, n], zr.at[chunk, n], mirror)
                   for n, (src, r, c) in enumerate(sketches)])
        zf.append([remote(r.at[:, mine, lo, i], r.at[:, mine, lo, i], zfs.at[chunk, n], zr.at[chunk, n], at(dzb=1))
                   for n, (src, r, c) in enumerate(sketches)])

    @pl.when(outer)
    def _():
        for c in (c for group in zc for c in group):
            c.start()

    yc, fc, xc = {}, {}, {}
    everything = pl.ds(0, 64)

    def forward(dy, part, half, i=everything):
        j = 2 * ((y - dy) % 4) + k
        fc[dy, part] = []
        for n, (src, r, c) in enumerate(sketches):
            if dy == 0:
                source = src.at[:, s_me, i] if part == 0 else r.at[:, s_me, lo, i]
            else:
                source = c.at[:, j, half, i]
            fc[dy, part].append(remote(source, c.at[:, j, half, i], fs.at[dy, part, n], fr.at[dy, part, n], at(dk=1)))
        for c in fc[dy, part]:
            c.start()

    def columns(part, half, i=everything):
        for dy in (2, 1, 3):
            yc[dy, part] = []
            for n, (src, r, c) in enumerate(sketches):
                source = src.at[:, s_me, i] if part == 0 else r.at[:, s_me, lo, i]
                yc[dy, part].append(remote(
                    source, c.at[:, j_me, half, i], ys.at[dy - 1, part, n], yr.at[dy - 1, part, n], at(dy=dy)))
            for c in yc[dy, part]:
                c.start()

    def rows(dx, chunk):
        i = rows_of[chunk]
        xc[dx, chunk] = [remote(r.at[:, mine, lo, i], r.at[:, mine, lo, i], xs.at[dx - 1, chunk, n], xr.at[dx - 1, chunk, n],
                                at(dx=dx)) for n, (src, r, c) in enumerate(sketches)]
        for c in xc[dx, chunk]:
            c.start()

    columns(0, hi)
    forward(0, 0, hi)

    tlocal.wait()
    tcopy.wait_recv()
    sq[...] = tbuf[...].reshape(128, 128).T
    half_at = pl.multiple_of((q % 2) * 64, 64)
    res[...] = sq[pl.ds(half_at, 64), :].reshape(res.shape)
    def slot(d):
        return pl.ds((2 * d[0] + d[1]) * 128, 128)

    def gather_copies(p, h):
        return [remote(xbuf.at[p, h, :, slot((0, 0))], xbuf.at[p, h, :, slot(d)], ags.at[p, h, n], agr.at[p, h, n],
                       at(dy=d[0], dk=d[1])) for n, d in enumerate(gathers)]

    def gather(p, h):
        xbuf[p, h, :, slot((0, 0))] = jnp.tanh(res[h]).astype(jnp.bfloat16)
        for c in gather_copies(p, h):
            c.start()

    for h in range(PARTS):
        gather(0, h)

    for chunk, i in enumerate(rows_of):
        for c in zc[chunk]:
            c.wait_recv()

        @pl.when(outer)
        def _():
            for passed in zf[chunk]:
                passed.start()

        for dx in (2, 1, 3):
            rows(dx, chunk)
        columns(1 + chunk, lo, i)
        forward(0, 1 + chunk, lo, i)
        if chunk == 1:
            for dy in (1, 3, 2):
                for c in yc[dy, 0]:
                    c.wait_recv()
                forward(dy, 0, hi)
    for n, (src, r, c) in enumerate(sketches):
        own = pltpu.make_async_copy(r.at[:, s_me, lo], c.at[:, j_me, lo], lsem.at[3, n])
        own.start()
        local.append(own)
    for chunk, i in enumerate(rows_of):
        for dy in (1, 3, 2):
            for c in yc[dy, 1 + chunk]:
                c.wait_recv()
            forward(dy, 1 + chunk, lo, i)
    for c in local:
        c.wait()
    for group in fc.values():
        for c in group:
            c.wait_recv()

    for dx in (0, 1, 3, 2):
        if dx:
            for chunk in range(CHUNKS):
                for c in xc[dx, chunk]:
                    c.wait_recv()
        to = (4 - dx) % 4
        lanes = pl.ds(to * 256, 256)
        right_at = [2 * ((x - dx) % 4) + zb, 2 * ((x - dx) % 4) + 1 - zb]
        for dy in range(4):
            left_at = [2 * ((y - dy) % 4) + k, 2 * ((y - dy) % 4) + 1 - k]
            total = jnp.zeros((256, 256), jnp.float32)
            for layer in range(2):
                grams = []
                for src, r, c in sketches:
                    left = jnp.concatenate([c[layer, j].reshape(128, 256) for j in left_at], axis=0)
                    right = jnp.concatenate([r[layer, j].reshape(128, 256) for j in right_at], axis=0)
                    grams.append(lax.dot_general(left, right, (((1,), (1,)), ((), ())), preferred_element_type=jnp.float32))
                total = total + grams[0] * grams[1]
            kt[pl.ds(dy * 256, 256), lanes] = (total * inv_scale).astype(jnp.bfloat16)

    def step(p, last=False):
        gathered, copies = [], []
        for h in range(PARTS):
            gathered.append(gather_copies(p, h))
            for c in reversed(gathered[h]):
                c.wait_recv()
            part = jnp.dot(xbuf[p, h], kt[...], preferred_element_type=jnp.float32)
            yloc[h] = part[:, 0:128]
            copies.append([])
            for n, (dx, dz) in enumerate(sums):
                lane = (2 * dx + dz) * 128
                rsend[p, h, n] = part[:, lane:lane + 128].astype(jnp.bfloat16)
                copies[h].append(remote(
                    rsend.at[p, h, n], rrecv.at[p, h, n], rss.at[p, h, n], rsr.at[p, h, n], at(dx=dx, dzb=dz)))
            for c in copies[h]:
                c.start()
        for c in (c for group in gathered for c in group):
            c.wait_send()
        for h in range(PARTS):
            for c in reversed(copies[h]):
                c.wait_recv()
            total = yloc[h]
            for n in range(7):
                total = total + rrecv[p, h, n].astype(jnp.float32)
            res[h] = res[h] - RATE * total
            if not last:
                gather(1 - p, h)
        for c in (c for group in copies for c in group):
            c.wait_send()

    def pair(_, carry):
        step(0)
        step(1)
        return carry

    lax.fori_loop(0, ITERS // 2 - 1, pair, 0)
    step(0)
    step(1, last=True)

    sq[...] = jnp.zeros_like(sq)
    sq[pl.ds(half_at, 64), :] = res[...].reshape(64, 128)
    osend[...] = sq[...].T
    for h in range(2):
        for e in range(2):
            n = 2 * h + e
            z_to = 4 * h + 2 * zb + e
            piece = osend.at[pl.ds(h * 64 + e * 32, 32)]

            @pl.when(z_to != z)
            def _():
                remote(piece, orecv.at[q], oss.at[n], osr.at[q], place(x, y, z_to, k)).start()

            @pl.when(z_to == z)
            def _():
                pltpu.make_async_copy(piece, orecv.at[q], osr.at[q]).start()
    tcopy.wait_send()

    @pl.when(outer)
    def _():
        for c in (c for group in (*zc, *zf) for c in group):
            c.wait_send()

    for group in (*yc.values(), *fc.values(), *xc.values()):
        for c in group:
            c.wait_send()

    for n in range(4):
        pltpu.make_async_copy(osend.at[pl.ds(0, 32)], orecv.at[n], osr.at[n]).wait()
    out[:, 0:128] = orecv[0] + orecv[1]
    out[:, 128:256] = orecv[2] + orecv[3]
    for h in range(2):
        for e in range(2):
            n = 2 * h + e
            z_to = 4 * h + 2 * zb + e
            piece = osend.at[pl.ds(h * 64 + e * 32, 32)]

            @pl.when(z_to != z)
            def _():
                remote(piece, orecv.at[q], oss.at[n], osr.at[q], place(x, y, z_to, k)).wait_send()


def body(act_sketch, grad_sketch, targets):
    layers, examples, width = act_sketch.shape
    inv_scale = 4.0 / (width * math.sqrt(examples * lax.axis_size("row")))
    bf16, f32 = jnp.bfloat16, jnp.float32
    dma = pltpu.SemaphoreType.DMA
    hbm = pl.BlockSpec(memory_space=pltpu.HBM)
    return pl.pallas_call(
        functools.partial(kernel, inv_scale),
        name="descent",
        out_shape=jax.ShapeDtypeStruct((32, 256), f32),
        in_specs=[hbm, hbm, hbm],
        out_specs=pl.BlockSpec(memory_space=pltpu.VMEM),
        scratch_shapes=[
            *[pltpu.VMEM((2, 8, 2, 64, 256), bf16)] * 4,
            pltpu.VMEM((1024, 1024), bf16),
            pltpu.VMEM((2, PARTS, 64 // PARTS, 1024), bf16),
            pltpu.VMEM((2, PARTS, 7, 64 // PARTS, 128), bf16),
            pltpu.VMEM((2, PARTS, 7, 64 // PARTS, 128), bf16),
            pltpu.VMEM((PARTS, 64 // PARTS, 128), f32),
            pltpu.VMEM((PARTS, 64 // PARTS, 128), f32),
            pltpu.VMEM((2, 64, 128), f32),
            pltpu.VMEM((128, 128), f32),
            pltpu.VMEM((128, 128), f32),
            pltpu.VMEM((4, 32, 128), f32),
            dma((4, 2)),
            dma((CHUNKS, 2)), dma((CHUNKS, 2)), dma((CHUNKS, 2)),
            dma(()), dma(()),
            dma((3, CHUNKS, 2)), dma((3, CHUNKS, 2)),
            dma((3, 1 + CHUNKS, 2)), dma((3, 1 + CHUNKS, 2)),
            dma((4, 1 + CHUNKS, 2)), dma((4, 1 + CHUNKS, 2)),
            dma((2, PARTS, 7)), dma((2, PARTS, 7)),
            dma((2, PARTS, 7)), dma((2, PARTS, 7)),
            dma((4,)), dma((4,)),
        ],
        compiler_params=pltpu.CompilerParams(collective_id=0, has_side_effects=True, vmem_limit_bytes=40 * 2**20),
    )(*[pltpu.with_memory_space_constraint(v, pltpu.HBM) for v in (act_sketch.reshape(layers, 8, 64, width), grad_sketch.reshape(layers, 8, 64, width),
      targets.reshape(8, 64, targets.shape[1]))])


def solution(mesh):
    return jax.shard_map(
        body,
        mesh=mesh,
        in_specs=(P(None, "row", None), P(None, "row", None), P("row", None)),
        out_specs=P(("row", "col"), None),
        check_vma=False,
    )
```

```python
import functools
import math

import jax
import jax.numpy as jnp
from jax import lax
from jax.experimental import pallas as pl
from jax.experimental.pallas import tpu as pltpu
from jax.sharding import PartitionSpec as P

ITERS = 8
SIZES = (16, 16, 16, 16)
CHUNKS = len(SIZES)
PARTS = 4
ORDER = ((2, 3), (0, 1))
RATE = 0.05
MESH = pl.DeviceIdType.MESH


def place(x, y, z, k):
    return ((z // 4) * 8 + y * 2 + k, x * 4 + z % 4)


def kernel(inv_scale, act, grad, tgt, out, ra, rg, ca, cg, kt, xbuf, rsend, rrecv, yloc, res, tbuf, sq, osend, orecv,
           lsem, zs, zfs, zr, ts, tr, xs, xr, ys, yr, fs, fr, rss, rsr, ags, agr, oss, osr):
    row, col = lax.axis_index("row"), lax.axis_index("col")
    x, zlo = col // 4, col % 4
    hi, y, k = row // 8, (row // 2) % 4, row % 2
    z = hi * 4 + zlo
    zb = z % 2
    q = z // 2
    s_me = 2 * x + zb
    j_me = 2 * y + k
    sketches = ((act, ra, ca), (grad, rg, cg))

    def at(dx=0, dy=0, dzb=0, dk=0):
        return place((x + dx) % 4, (y + dy) % 4, z + dzb * (1 - 2 * zb), k + dk * (1 - 2 * k))

    def remote(src, dst, ssem, rsem, device):
        return pltpu.make_async_remote_copy(
            src_ref=src, dst_ref=dst, send_sem=ssem, recv_sem=rsem, device_id=device, device_id_type=MESH)

    local = []
    for n, (src, r, c) in enumerate(sketches):
        local.append(pltpu.make_async_copy(src, r.at[:, :, 0], lsem.at[0, n]))
        local.append(pltpu.make_async_copy(src.at[:, s_me], c.at[:, j_me, 0], lsem.at[1, n]))
    tcols = pl.ds(pl.multiple_of((q // 2) * 128, 128), 128)
    tlocal = pltpu.make_async_copy(tgt.at[s_me, :, tcols], tbuf.at[0], lsem.at[2, 0])
    for c in local:
        c.start()
    tlocal.start()

    sums = [(dx, dz) for dx in (2, 1, 3, 0) for dz in (1, 0) if (dx, dz) != (0, 0)]
    gathers = [(dy, dk) for dy in (2, 1, 3, 0) for dk in (1, 0) if (dy, dk) != (0, 0)]
    barrier = pltpu.get_barrier_semaphore()

    def greet(device):
        pl.semaphore_signal(barrier, inc=1, device_id=device, device_id_type=MESH)

    for n in range(1, 4):
        for b in range(2):
            greet(place(x, y, 2 * ((q + n) % 4) + b, k))
    for dx, dz in sums:
        greet(at(dx=dx, dzb=dz))
    for dy, dk in gathers:
        greet(at(dy=dy, dk=dk))
    pl.semaphore_wait(barrier, len(sums) + len(gathers) + 6)

    mirror = place(x, y, 7 - z, k)
    s_mirror = 2 * x + 1 - zb
    mcols = pl.ds(pl.multiple_of(((3 - q) // 2) * 128, 128), 128)
    tcopy = remote(tgt.at[s_mirror, :, mcols], tbuf.at[1], ts, tr, mirror)
    tcopy.start()
    outer = zlo % 3 == 0
    mine = pl.ds(2 * x, 2)
    rows_of = [pl.ds(sum(SIZES[:c]), SIZES[c]) for c in range(CHUNKS)]
    zc, zf = [], []
    for chunk, i in enumerate(rows_of):
        zc.append([remote(src.at[:, mine, i], r.at[:, mine, 1, i], zs.at[chunk, n], zr.at[chunk, n], mirror)
                   for n, (src, r, c) in enumerate(sketches)])
        zf.append([remote(r.at[:, mine, 1, i], r.at[:, mine, 1, i], zfs.at[chunk, n], zr.at[chunk, n], at(dzb=1))
                   for n, (src, r, c) in enumerate(sketches)])

    @pl.when(outer)
    def _():
        for c in (c for group in zc for c in group):
            c.start()

    yc, fc, xc = {}, {}, {}
    everything = pl.ds(0, 64)

    def forward(dy, part, half, i=everything):
        j = 2 * ((y - dy) % 4) + k
        fc[dy, part] = []
        for n, (src, r, c) in enumerate(sketches):
            if dy == 0:
                source = src.at[:, s_me, i] if part == 0 else r.at[:, s_me, 1, i]
            else:
                source = c.at[:, j, half, i]
            fc[dy, part].append(remote(source, c.at[:, j, half, i], fs.at[dy, part, n], fr.at[dy, part, n], at(dk=1)))
        for c in fc[dy, part]:
            c.start()

    def columns(part, half, i=everything):
        for dy in (2, 1, 3):
            yc[dy, part] = []
            for n, (src, r, c) in enumerate(sketches):
                source = src.at[:, s_me, i] if part == 0 else r.at[:, s_me, 1, i]
                yc[dy, part].append(remote(
                    source, c.at[:, j_me, half, i], ys.at[dy - 1, part, n], yr.at[dy - 1, part, n], at(dy=dy)))
            for c in yc[dy, part]:
                c.start()

    def rows(dx, chunk):
        i = rows_of[chunk]
        xc[dx, chunk] = [remote(r.at[:, mine, 1, i], r.at[:, mine, 1, i], xs.at[dx - 1, chunk, n], xr.at[dx - 1, chunk, n],
                                at(dx=dx)) for n, (src, r, c) in enumerate(sketches)]
        for c in xc[dx, chunk]:
            c.start()

    columns(0, 0)
    forward(0, 0, 0)

    tlocal.wait()
    tcopy.wait_recv()
    sq[...] = tbuf[...].reshape(128, 128).T
    half_at = pl.multiple_of((q % 2) * 64, 64)
    res[...] = sq[pl.ds(half_at, 64), :].reshape(res.shape)
    def slot(d):
        return pl.ds((2 * d[0] + d[1]) * 128, 128)

    def gather_copies(p, h):
        return [remote(xbuf.at[p, h, :, slot((0, 0))], xbuf.at[p, h, :, slot(d)], ags.at[p, h, n], agr.at[p, h, n],
                       at(dy=d[0], dk=d[1])) for n, d in enumerate(gathers)]

    def gather(p, h):
        xbuf[p, h, :, slot((0, 0))] = jnp.tanh(res[h]).astype(jnp.bfloat16)
        for c in gather_copies(p, h):
            c.start()

    for h in range(PARTS):
        gather(0, h)

    for chunk, i in enumerate(rows_of):
        for c in zc[chunk]:
            c.wait_recv()

        @pl.when(outer)
        def _():
            for passed in zf[chunk]:
                passed.start()

        for dx in (2, 1, 3):
            rows(dx, chunk)
        columns(1 + chunk, 1, i)
        forward(0, 1 + chunk, 1, i)
        if chunk == 1:
            for dy in (1, 3, 2):
                for c in yc[dy, 0]:
                    c.wait_recv()
                forward(dy, 0, 0)
    for n, (src, r, c) in enumerate(sketches):
        own = pltpu.make_async_copy(r.at[:, s_me, 1], c.at[:, j_me, 1], lsem.at[3, n])
        own.start()
        local.append(own)
    for chunk, i in enumerate(rows_of):
        for dy in (1, 3, 2):
            for c in yc[dy, 1 + chunk]:
                c.wait_recv()
            forward(dy, 1 + chunk, 1, i)
    for c in local:
        c.wait()
    for group in fc.values():
        for c in group:
            c.wait_recv()

    first_lanes = lax.broadcasted_iota(jnp.int32, (256, 128), 1) < 64

    def products(half, dy, places):
        left_at = [2 * ((y - dy) % 4) + k, 2 * ((y - dy) % 4) + 1 - k]
        total = jnp.zeros((256, 64 * len(places)), jnp.float32)
        for layer in range(2):
            grams = []
            for src, r, c in sketches:
                left = jnp.concatenate([c[layer, j].reshape(128, 256) for j in left_at], axis=0)
                right = jnp.concatenate(
                    [r[layer, 2 * ((x + dx) % 4) + (zb if dz == 0 else 1 - zb), half] for dx, dz in places], axis=0)
                grams.append(lax.dot_general(left, right, (((1,), (1,)), ((), ())), preferred_element_type=jnp.float32))
            total = total + grams[0] * grams[1]
        return total * inv_scale

    def place_own(dxs):
        for dy in range(4):
            block = products(0, dy, [(dx, dz) for dx in dxs for dz in range(2)])
            for m, dx in enumerate(dxs):
                pair = block[:, m * 128:(m + 1) * 128]
                kt[dy * 256:(dy + 1) * 256, dx * 256:dx * 256 + 128] = pair.astype(jnp.bfloat16)
                kt[dy * 256:(dy + 1) * 256, dx * 256 + 128:dx * 256 + 256] = pltpu.roll(pair, 64, 1).astype(jnp.bfloat16)

    def place_other(dxs):
        for dy in range(4):
            block = products(1, dy, [(dx, dz) for dx in dxs for dz in range(2)])
            for m, dx in enumerate(dxs):
                pair = block[:, m * 128:(m + 1) * 128]
                for dz, value in ((0, pltpu.roll(pair, 64, 1)), (1, pair)):
                    at_k = kt.at[pl.ds(dy * 256, 256), pl.ds(dx * 256 + dz * 128, 128)]
                    at_k[...] = jnp.where(first_lanes, at_k[...].astype(jnp.float32), value).astype(jnp.bfloat16)

    place_own((0, 1))
    place_own((2, 3))
    place_other((0,))
    for dxs in ((1, 3, 2),):
        for dx in dxs:
            for chunk in range(CHUNKS):
                for c in xc[dx, chunk]:
                    c.wait_recv()
        place_other([(4 - dx) % 4 for dx in dxs])

    def step(p, last=False):
        gathered, copies = [], []
        for h in range(PARTS):
            gathered.append(gather_copies(p, h))
            for c in reversed(gathered[h]):
                c.wait_recv()
            copies.append([None] * len(sums))
            for dxs in ORDER:
                part = jnp.dot(xbuf[p, h], kt[:, dxs[0] * 256:(dxs[-1] + 1) * 256], preferred_element_type=jnp.float32)
                for m, (dx, dz) in enumerate((dx, dz) for dx in dxs for dz in range(2)):
                    piece = part[:, m * 128:(m + 1) * 128]
                    if (dx, dz) == (0, 0):
                        yloc[h] = piece
                        continue
                    n = sums.index((dx, dz))
                    rsend[p, h, n] = piece.astype(jnp.bfloat16)
                    copies[h][n] = remote(
                        rsend.at[p, h, n], rrecv.at[p, h, n], rss.at[p, h, n], rsr.at[p, h, n], at(dx=dx, dzb=dz))
                for n, (dx, dz) in enumerate(sums):
                    if dx in dxs:
                        copies[h][n].start()
        for c in (c for group in gathered for c in group):
            c.wait_send()
        for h in range(PARTS):
            for c in reversed(copies[h]):
                c.wait_recv()
            total = yloc[h]
            for n in range(7):
                total = total + rrecv[p, h, n].astype(jnp.float32)
            res[h] = res[h] - RATE * total
            if not last:
                gather(1 - p, h)
        for c in (c for group in copies for c in group):
            c.wait_send()

    def pair(_, carry):
        step(0)
        step(1)
        return carry

    lax.fori_loop(0, ITERS // 2 - 1, pair, 0)
    step(0)
    step(1, last=True)

    sq[...] = jnp.zeros_like(sq)
    sq[pl.ds(half_at, 64), :] = res[...].reshape(64, 128)
    osend[...] = sq[...].T
    for h in range(2):
        for e in range(2):
            n = 2 * h + e
            z_to = 4 * (hi if h == 0 else 1 - hi) + 2 * zb + e
            piece = osend.at[pl.ds(h * 64 + e * 32, 32)]

            @pl.when(z_to != z)
            def _():
                remote(piece, orecv.at[q], oss.at[n], osr.at[q], place(x, y, z_to, k)).start()

            @pl.when(z_to == z)
            def _():
                pltpu.make_async_copy(piece, orecv.at[q], osr.at[q]).start()
    tcopy.wait_send()

    @pl.when(outer)
    def _():
        for c in (c for group in (*zc, *zf) for c in group):
            c.wait_send()

    for group in (*yc.values(), *fc.values(), *xc.values()):
        for c in group:
            c.wait_send()

    for n in range(4):
        pltpu.make_async_copy(osend.at[pl.ds(0, 32)], orecv.at[n], osr.at[n]).wait()
    out[:, 0:128] = orecv[0] + orecv[1]
    out[:, 128:256] = orecv[2] + orecv[3]
    for h in range(2):
        for e in range(2):
            n = 2 * h + e
            z_to = 4 * (hi if h == 0 else 1 - hi) + 2 * zb + e
            piece = osend.at[pl.ds(h * 64 + e * 32, 32)]

            @pl.when(z_to != z)
            def _():
                remote(piece, orecv.at[q], oss.at[n], osr.at[q], place(x, y, z_to, k)).wait_send()


def body(act_sketch, grad_sketch, targets):
    layers, examples, width = act_sketch.shape
    inv_scale = 4.0 / (width * math.sqrt(examples * lax.axis_size("row")))
    bf16, f32 = jnp.bfloat16, jnp.float32
    dma = pltpu.SemaphoreType.DMA
    hbm = pl.BlockSpec(memory_space=pltpu.HBM)
    return pl.pallas_call(
        functools.partial(kernel, inv_scale),
        name="descent",
        out_shape=jax.ShapeDtypeStruct((32, 256), f32),
        in_specs=[hbm, hbm, hbm],
        out_specs=pl.BlockSpec(memory_space=pltpu.VMEM),
        scratch_shapes=[
            *[pltpu.VMEM((2, 8, 2, 64, 256), bf16)] * 4,
            pltpu.VMEM((1024, 1024), bf16),
            pltpu.VMEM((2, PARTS, 64 // PARTS, 1024), bf16),
            pltpu.VMEM((2, PARTS, 7, 64 // PARTS, 128), bf16),
            pltpu.VMEM((2, PARTS, 7, 64 // PARTS, 128), bf16),
            pltpu.VMEM((PARTS, 64 // PARTS, 128), f32),
            pltpu.VMEM((PARTS, 64 // PARTS, 128), f32),
            pltpu.VMEM((2, 64, 128), f32),
            pltpu.VMEM((128, 128), f32),
            pltpu.VMEM((128, 128), f32),
            pltpu.VMEM((4, 32, 128), f32),
            dma((4, 2)),
            dma((CHUNKS, 2)), dma((CHUNKS, 2)), dma((CHUNKS, 2)),
            dma(()), dma(()),
            dma((3, CHUNKS, 2)), dma((3, CHUNKS, 2)),
            dma((3, 1 + CHUNKS, 2)), dma((3, 1 + CHUNKS, 2)),
            dma((4, 1 + CHUNKS, 2)), dma((4, 1 + CHUNKS, 2)),
            dma((2, PARTS, 7)), dma((2, PARTS, 7)),
            dma((2, PARTS, 7)), dma((2, PARTS, 7)),
            dma((4,)), dma((4,)),
        ],
        compiler_params=pltpu.CompilerParams(collective_id=0, has_side_effects=True, vmem_limit_bytes=40 * 2**20),
    )(*[pltpu.with_memory_space_constraint(v, pltpu.HBM) for v in (act_sketch.reshape(layers, 8, 64, width), grad_sketch.reshape(layers, 8, 64, width),
      targets.reshape(8, 64, targets.shape[1]))])


def solution(mesh):
    return jax.shard_map(
        body,
        mesh=mesh,
        in_specs=(P(None, "row", None), P(None, "row", None), P("row", None)),
        out_specs=P(("row", "col"), None),
        check_vma=False,
    )
```

```python
import functools
import math

import jax
import jax.numpy as jnp
from jax import lax
from jax.experimental import pallas as pl
from jax.experimental.pallas import tpu as pltpu
from jax.sharding import PartitionSpec as P

ITERS = 8
SIZES = (16, 16, 16, 16)
CHUNKS = len(SIZES)
PARTS = 4
ORDER = ((2, 3), (0, 1))
RATE = 0.05
MESH = pl.DeviceIdType.MESH


def place(x, y, z, k):
    return ((z // 4) * 8 + y * 2 + k, x * 4 + z % 4)


def kernel(inv_scale, act, grad, tgt, out, ra, rg, ca, cg, kt, xbuf, rsend, rrecv, yloc, res, tbuf, sq, osend, orecv,
           lsem, zs, zfs, zr, ts, tr, xs, xr, ys, yr, fs, fr, rss, rsr, ags, agr, oss, osr):
    row, col = lax.axis_index("row"), lax.axis_index("col")
    x, zlo = col // 4, col % 4
    hi, y, k = row // 8, (row // 2) % 4, row % 2
    z = hi * 4 + zlo
    zb = z % 2
    q = z // 2
    s_me = 2 * x + zb
    j_me = 2 * y + k
    sketches = ((act, ra, ca), (grad, rg, cg))

    def at(dx=0, dy=0, dzb=0, dk=0):
        return place((x + dx) % 4, (y + dy) % 4, z + dzb * (1 - 2 * zb), k + dk * (1 - 2 * k))

    def remote(src, dst, ssem, rsem, device):
        return pltpu.make_async_remote_copy(
            src_ref=src, dst_ref=dst, send_sem=ssem, recv_sem=rsem, device_id=device, device_id_type=MESH)

    local = []
    for n, (src, r, c) in enumerate(sketches):
        local.append(pltpu.make_async_copy(src, r.at[:, :, 0], lsem.at[0, n]))
        local.append(pltpu.make_async_copy(src.at[:, s_me], c.at[:, j_me, 0], lsem.at[1, n]))
    tcols = pl.ds(pl.multiple_of((q // 2) * 128, 128), 128)
    tlocal = pltpu.make_async_copy(tgt.at[s_me, :, tcols], tbuf.at[0], lsem.at[2, 0])
    for c in local:
        c.start()
    tlocal.start()

    sums = [(dx, dz) for dx in (2, 1, 3, 0) for dz in (1, 0) if (dx, dz) != (0, 0)]
    gathers = [(dy, dk) for dy in (2, 1, 3, 0) for dk in (1, 0) if (dy, dk) != (0, 0)]
    barrier = pltpu.get_barrier_semaphore()

    def greet(device):
        pl.semaphore_signal(barrier, inc=1, device_id=device, device_id_type=MESH)

    for n in range(1, 4):
        for b in range(2):
            greet(place(x, y, 2 * ((q + n) % 4) + b, k))
    near = [(dx, dz) for dx, dz in sums if 0 in (dx, dz)]
    beside = [(dy, dk) for dy, dk in gathers if 0 in (dy, dk)]
    for dx, dz in near:
        greet(at(dx=dx, dzb=dz))
    for dy, dk in beside:
        greet(at(dy=dy, dk=dk))
    pl.semaphore_wait(barrier, len(near) + len(beside) + 6)

    mirror = place(x, y, 7 - z, k)
    s_mirror = 2 * x + 1 - zb
    mcols = pl.ds(pl.multiple_of(((3 - q) // 2) * 128, 128), 128)
    tcopy = remote(tgt.at[s_mirror, :, mcols], tbuf.at[1], ts, tr, mirror)
    tcopy.start()
    outer = zlo % 3 == 0
    mine = pl.ds(2 * x, 2)
    rows_of = [pl.ds(sum(SIZES[:c]), SIZES[c]) for c in range(CHUNKS)]
    zc, zf = [], []
    for chunk, i in enumerate(rows_of):
        zc.append([remote(src.at[:, mine, i], r.at[:, mine, 1, i], zs.at[chunk, n], zr.at[chunk, n], mirror)
                   for n, (src, r, c) in enumerate(sketches)])
        zf.append([remote(r.at[:, mine, 1, i], r.at[:, mine, 1, i], zfs.at[chunk, n], zr.at[chunk, n], at(dzb=1))
                   for n, (src, r, c) in enumerate(sketches)])

    @pl.when(outer)
    def _():
        for c in (c for group in zc for c in group):
            c.start()

    yc, fc, xc = {}, {}, {}
    everything = pl.ds(0, 64)

    def forward(dy, part, half, i=everything):
        j = 2 * ((y - dy) % 4) + k
        fc[dy, part] = []
        for n, (src, r, c) in enumerate(sketches):
            if dy == 0:
                source = src.at[:, s_me, i] if part == 0 else r.at[:, s_me, 1, i]
            else:
                source = c.at[:, j, half, i]
            fc[dy, part].append(remote(source, c.at[:, j, half, i], fs.at[dy, part, n], fr.at[dy, part, n], at(dk=1)))
        for c in fc[dy, part]:
            c.start()

    def columns(part, half, i=everything):
        for dy in (2, 1, 3):
            yc[dy, part] = []
            for n, (src, r, c) in enumerate(sketches):
                source = src.at[:, s_me, i] if part == 0 else r.at[:, s_me, 1, i]
                yc[dy, part].append(remote(
                    source, c.at[:, j_me, half, i], ys.at[dy - 1, part, n], yr.at[dy - 1, part, n], at(dy=dy)))
            for c in yc[dy, part]:
                c.start()

    def rows(dx, chunk):
        i = rows_of[chunk]
        xc[dx, chunk] = [remote(r.at[:, mine, 1, i], r.at[:, mine, 1, i], xs.at[dx - 1, chunk, n], xr.at[dx - 1, chunk, n],
                                at(dx=dx)) for n, (src, r, c) in enumerate(sketches)]
        for c in xc[dx, chunk]:
            c.start()

    columns(0, 0)
    forward(0, 0, 0)

    tlocal.wait()
    tcopy.wait_recv()
    sq[...] = tbuf[...].reshape(128, 128).T
    half_at = pl.multiple_of((q % 2) * 64, 64)
    res[...] = sq[pl.ds(half_at, 64), :].reshape(res.shape)
    def slot(d):
        return pl.ds((2 * d[0] + d[1]) * 128, 128)

    def gather_copies(p, h):
        return [remote(xbuf.at[p, h, :, slot((0, 0))], xbuf.at[p, h, :, slot(d)], ags.at[p, h, n], agr.at[p, h, n],
                       at(dy=d[0], dk=d[1])) for n, d in enumerate(gathers)]

    def gather(p, h):
        xbuf[p, h, :, slot((0, 0))] = jnp.tanh(res[h]).astype(jnp.bfloat16)
        for c in gather_copies(p, h):
            c.start()


    for chunk, i in enumerate(rows_of):
        for c in zc[chunk]:
            c.wait_recv()

        @pl.when(outer)
        def _():
            for passed in zf[chunk]:
                passed.start()

        for dx in (2, 1, 3):
            rows(dx, chunk)
        columns(1 + chunk, 1, i)
        forward(0, 1 + chunk, 1, i)
        if chunk == 1:
            for dy in (1, 3, 2):
                for c in yc[dy, 0]:
                    c.wait_recv()
                forward(dy, 0, 0)
            for h in range(PARTS):
                gather(0, h)
    for n, (src, r, c) in enumerate(sketches):
        own = pltpu.make_async_copy(r.at[:, s_me, 1], c.at[:, j_me, 1], lsem.at[3, n])
        own.start()
        local.append(own)
    for chunk, i in enumerate(rows_of):
        for dy in (1, 3, 2):
            for c in yc[dy, 1 + chunk]:
                c.wait_recv()
            forward(dy, 1 + chunk, 1, i)
    for c in local:
        c.wait()
    for group in fc.values():
        for c in group:
            c.wait_recv()

    first_lanes = lax.broadcasted_iota(jnp.int32, (256, 128), 1) < 64

    def products(half, dy, places):
        left_at = [2 * ((y - dy) % 4) + k, 2 * ((y - dy) % 4) + 1 - k]
        total = jnp.zeros((256, 64 * len(places)), jnp.float32)
        for layer in range(2):
            grams = []
            for src, r, c in sketches:
                left = jnp.concatenate([c[layer, j].reshape(128, 256) for j in left_at], axis=0)
                right = jnp.concatenate(
                    [r[layer, 2 * ((x + dx) % 4) + (zb if dz == 0 else 1 - zb), half] for dx, dz in places], axis=0)
                grams.append(lax.dot_general(left, right, (((1,), (1,)), ((), ())), preferred_element_type=jnp.float32))
            total = total + grams[0] * grams[1]
        return total * inv_scale

    def place_own(dxs):
        for dy in range(4):
            block = products(0, dy, [(dx, dz) for dx in dxs for dz in range(2)])
            for m, dx in enumerate(dxs):
                pair = block[:, m * 128:(m + 1) * 128]
                kt[dy * 256:(dy + 1) * 256, dx * 256:dx * 256 + 128] = pair.astype(jnp.bfloat16)
                kt[dy * 256:(dy + 1) * 256, dx * 256 + 128:dx * 256 + 256] = pltpu.roll(pair, 64, 1).astype(jnp.bfloat16)

    def place_other(dxs):
        for dy in range(4):
            block = products(1, dy, [(dx, dz) for dx in dxs for dz in range(2)])
            for m, dx in enumerate(dxs):
                pair = block[:, m * 128:(m + 1) * 128]
                for dz, value in ((0, pltpu.roll(pair, 64, 1)), (1, pair)):
                    at_k = kt.at[pl.ds(dy * 256, 256), pl.ds(dx * 256 + dz * 128, 128)]
                    at_k[...] = jnp.where(first_lanes, at_k[...].astype(jnp.float32), value).astype(jnp.bfloat16)

    place_own((0, 1))
    place_own((2, 3))
    place_other((0,))
    for dxs in ((1, 3, 2),):
        for dx in dxs:
            for chunk in range(CHUNKS):
                for c in xc[dx, chunk]:
                    c.wait_recv()
        place_other([(4 - dx) % 4 for dx in dxs])

    def step(p, last=False):
        gathered, copies = [], []
        for h in range(PARTS):
            gathered.append(gather_copies(p, h))
            for c in reversed(gathered[h]):
                c.wait_recv()
            copies.append([None] * len(sums))
            for dxs in ORDER:
                part = jnp.dot(xbuf[p, h], kt[:, dxs[0] * 256:(dxs[-1] + 1) * 256], preferred_element_type=jnp.float32)
                for m, (dx, dz) in enumerate((dx, dz) for dx in dxs for dz in range(2)):
                    piece = part[:, m * 128:(m + 1) * 128]
                    if (dx, dz) == (0, 0):
                        yloc[h] = piece
                        continue
                    n = sums.index((dx, dz))
                    rsend[p, h, n] = piece.astype(jnp.bfloat16)
                    copies[h][n] = remote(
                        rsend.at[p, h, n], rrecv.at[p, h, n], rss.at[p, h, n], rsr.at[p, h, n], at(dx=dx, dzb=dz))
                for n, (dx, dz) in enumerate(sums):
                    if dx in dxs:
                        copies[h][n].start()
        for c in (c for group in gathered for c in group):
            c.wait_send()
        for h in range(PARTS):
            for c in reversed(copies[h]):
                c.wait_recv()
            total = yloc[h]
            for n in range(7):
                total = total + rrecv[p, h, n].astype(jnp.float32)
            res[h] = res[h] - RATE * total
            if not last:
                gather(1 - p, h)
        for c in (c for group in copies for c in group):
            c.wait_send()

    def pair(_, carry):
        step(0)
        step(1)
        return carry

    lax.fori_loop(0, ITERS // 2 - 1, pair, 0)
    step(0)
    step(1, last=True)

    sq[...] = jnp.zeros_like(sq)
    sq[pl.ds(half_at, 64), :] = res[...].reshape(64, 128)
    osend[...] = sq[...].T
    for h in range(2):
        for e in range(2):
            n = 2 * h + e
            z_to = 4 * (hi if h == 0 else 1 - hi) + 2 * zb + e
            piece = osend.at[pl.ds(h * 64 + e * 32, 32)]

            @pl.when(z_to != z)
            def _():
                remote(piece, orecv.at[q], oss.at[n], osr.at[q], place(x, y, z_to, k)).start()

            @pl.when(z_to == z)
            def _():
                pltpu.make_async_copy(piece, orecv.at[q], osr.at[q]).start()
    tcopy.wait_send()

    @pl.when(outer)
    def _():
        for c in (c for group in (*zc, *zf) for c in group):
            c.wait_send()

    for group in (*yc.values(), *fc.values(), *xc.values()):
        for c in group:
            c.wait_send()

    for n in range(4):
        pltpu.make_async_copy(osend.at[pl.ds(0, 32)], orecv.at[n], osr.at[n]).wait()
    out[:, 0:128] = orecv[0] + orecv[1]
    out[:, 128:256] = orecv[2] + orecv[3]
    for h in range(2):
        for e in range(2):
            n = 2 * h + e
            z_to = 4 * (hi if h == 0 else 1 - hi) + 2 * zb + e
            piece = osend.at[pl.ds(h * 64 + e * 32, 32)]

            @pl.when(z_to != z)
            def _():
                remote(piece, orecv.at[q], oss.at[n], osr.at[q], place(x, y, z_to, k)).wait_send()


def body(act_sketch, grad_sketch, targets):
    layers, examples, width = act_sketch.shape
    inv_scale = 4.0 / (width * math.sqrt(examples * lax.axis_size("row")))
    bf16, f32 = jnp.bfloat16, jnp.float32
    dma = pltpu.SemaphoreType.DMA
    hbm = pl.BlockSpec(memory_space=pltpu.HBM)
    return pl.pallas_call(
        functools.partial(kernel, inv_scale),
        name="descent",
        out_shape=jax.ShapeDtypeStruct((32, 256), f32),
        in_specs=[hbm, hbm, hbm],
        out_specs=pl.BlockSpec(memory_space=pltpu.VMEM),
        scratch_shapes=[
            *[pltpu.VMEM((2, 8, 2, 64, 256), bf16)] * 4,
            pltpu.VMEM((1024, 1024), bf16),
            pltpu.VMEM((2, PARTS, 64 // PARTS, 1024), bf16),
            pltpu.VMEM((2, PARTS, 7, 64 // PARTS, 128), bf16),
            pltpu.VMEM((2, PARTS, 7, 64 // PARTS, 128), bf16),
            pltpu.VMEM((PARTS, 64 // PARTS, 128), f32),
            pltpu.VMEM((PARTS, 64 // PARTS, 128), f32),
            pltpu.VMEM((2, 64, 128), f32),
            pltpu.VMEM((128, 128), f32),
            pltpu.VMEM((128, 128), f32),
            pltpu.VMEM((4, 32, 128), f32),
            dma((4, 2)),
            dma((CHUNKS, 2)), dma((CHUNKS, 2)), dma((CHUNKS, 2)),
            dma(()), dma(()),
            dma((3, CHUNKS, 2)), dma((3, CHUNKS, 2)),
            dma((3, 1 + CHUNKS, 2)), dma((3, 1 + CHUNKS, 2)),
            dma((4, 1 + CHUNKS, 2)), dma((4, 1 + CHUNKS, 2)),
            dma((2, PARTS, 7)), dma((2, PARTS, 7)),
            dma((2, PARTS, 7)), dma((2, PARTS, 7)),
            dma((4,)), dma((4,)),
        ],
        compiler_params=pltpu.CompilerParams(collective_id=0, has_side_effects=True, vmem_limit_bytes=40 * 2**20),
    )(*[pltpu.with_memory_space_constraint(v, pltpu.HBM) for v in (act_sketch.reshape(layers, 8, 64, width), grad_sketch.reshape(layers, 8, 64, width),
      targets.reshape(8, 64, targets.shape[1]))])


def solution(mesh):
    return jax.shard_map(
        body,
        mesh=mesh,
        in_specs=(P(None, "row", None), P(None, "row", None), P("row", None)),
        out_specs=P(("row", "col"), None),
        check_vma=False,
    )
```
